256 devices in a mesh: grp: 4 (over z_hi, core), dev: 64 (over x, y, z_lo).
Axes of the slice: x: 4, y: 4, z: 8 (z_hi: 2, z_lo: 4; z = z_hi * 4 + z_lo), core: 2. Of those that a mesh axis runs over, the one named last changes fastest.
Arguments:
- wavefield: float32 [256, 2, 128, 2048], P(('grp', 'dev')), may hold values from -6 to 6
- measured: float32 [256, 128, 2048], P(('grp', 'dev')), may hold values from 0.5 to 4
- leaf_map: float32 [256, 2, 128, 128], P(('grp', 'dev')), may hold values from -0.375 to 0.375
- factors: float32 [8, 256, 2, 128, 128], P(None, ('grp', 'dev')), may hold values from -0.375 to 0.375
- closing: float32 [256, 2, 128, 128], P(('grp', 'dev')), may hold values from -0.375 to 0.375
- box_perm: int32 [256, 2048], P(('grp', 'dev')), may hold values from 0 to 2047, each once within a row
- factor_order: int32 [8], replicated, may hold values from 0 to 7, each once
Outputs:
- projected: float32 [256, 2, 128, 2048], P(('grp', 'dev'))
The draws below stay inside these ranges and needn't reach their ends.
Inputs may be any that keep to these rules, and one draw needn't show every extreme that they name: `box_perm`: each row is a permutation of 0 .. 2047. `factor_order`: a permutation of 0 .. 7.
All inputs are finite; a program needn't handle non-finite values.
Results may differ from the reference program's by a relative error of at most 0.00018.
Values sent between devices are 32-bit elements; how exact they have to be, the bound alone decides.
A program may use at most 64 MiB of HBM per device.

```python
import math
import jax
import jax.numpy as jnp
from jax import lax

R = 64
K = 128
M = 128
Q = 2048
LEVELS = 8
SLABS = 256
N_DEV = 64


def level_of(rng, extent, shards, low, high):
    gain, own = 1.0, jax.random.fold_in(rng, 6)
    for dim, shards_of in shards:
        heights = jnp.exp(jax.random.uniform(jax.random.fold_in(own, dim), (shards_of,), jnp.float32, low / len(shards), high / len(shards)))
        gain = gain * jnp.repeat(heights, extent[dim] // shards_of).reshape([-1 if axis == dim else 1 for axis in range(len(extent))])
    return gain


def centred(key, shape, spread, limit, cuts=(), kind=jnp.bfloat16):
    loudness = level_of(key, shape, cuts, -0.22, 0.18) if cuts else 1.0
    drawn = jax.random.normal(key, shape, jnp.float32) * spread * loudness
    return jnp.minimum(jnp.maximum(drawn, -limit), limit).astype(kind)


def setup_inputs(seed: int = 0) -> dict:
    splits = jax.random.split(jax.random.key(seed), 8)
    return {
        "wavefield": centred(splits[0], (SLABS, 2, M, Q), 1.0, 6.0, ((0, 256),), jnp.float32),
        "measured": jnp.clip(jnp.exp(math.log(4.0) - 2.0794415 * jax.random.uniform(splits[1], (SLABS, M, Q), jnp.float32) ** level_of(splits[1], (SLABS, M, Q), ((0, 256),), -0.2, 0.2)), 0.5, 4.0),
        "leaf_map": centred(splits[2], (SLABS, 2, K, M), (2 * M) ** -0.5, 0.375, ((0, 256),), jnp.float32),
        "factors": centred(splits[3], (LEVELS, SLABS, 2, K, K), (2 * K) ** -0.5, 0.375, ((1, 256),), jnp.float32),
        "closing": centred(splits[4], (SLABS, 2, M, K), (2 * K) ** -0.5, 0.375, ((0, 256),), jnp.float32),
        "box_perm": jax.vmap(lambda own: jax.random.permutation(own, Q))(jax.random.split(splits[5], SLABS)).reshape((SLABS, Q)).astype(jnp.int32),
        "factor_order": jax.random.permutation(splits[6], LEVELS).astype(jnp.int32),
    }


def complex_product(matrix, vectors):
    highest = lax.Precision.HIGHEST
    real_part = jnp.einsum('pxy,pyz->pxz', matrix[:, 0], vectors[:, 0], precision=highest) - jnp.einsum('pxy,pyz->pxz', matrix[:, 1], vectors[:, 1], precision=highest)
    imag_part = jnp.einsum('pxy,pyz->pxz', matrix[:, 0], vectors[:, 1], precision=highest) + jnp.einsum('pxy,pyz->pxz', matrix[:, 1], vectors[:, 0], precision=highest)
    return jnp.stack([real_part, imag_part], axis=1)

def level_bit(level_at):
    dev_bits = N_DEV.bit_length() - 1
    if level_at < 2:
        return dev_bits + 1 - level_at
    return (level_at - 2) % dev_bits

def reference(wavefield, measured, leaf_map, factors, closing, box_perm, factor_order):
    coeffs = complex_product(leaf_map, wavefield)
    for level_at in range(LEVELS):
        bit_at = level_bit(level_at)
        shaped = coeffs.reshape(SLABS >> bit_at + 1, 2, 1 << bit_at, 2, 2, R, Q)
        coeffs = jnp.swapaxes(shaped, 1, 4).reshape(SLABS, 2, K, Q)
        coeffs = complex_product(factors[factor_order[level_at]], coeffs)
        if level_at == LEVELS // 2 - 1:
            coeffs = jnp.take_along_axis(coeffs, box_perm[:, None, None, :], axis=3)
    image = complex_product(closing, coeffs)
    modulus = jnp.sqrt(jnp.maximum(image[:, 0] * image[:, 0] + image[:, 1] * image[:, 1], 0.25))
    return measured[:, None] * image / modulus[:, None]
```

```python
import functools

import jax
import jax.numpy as jnp
from jax import lax
from jax.experimental import pallas as pl
from jax.experimental.pallas import tpu as pltpu
from jax.sharding import PartitionSpec as P

MESH = pl.DeviceIdType.MESH
LEVELS = 8
SWITCH = LEVELS // 2
WIDTH = 256
AHEAD = 2
LAG_A = 1
LAG_B = 1


def kernel(
    dev_bits, order_ref, perm_ref, field_hbm, measured_hbm, leaf_hbm, factors_hbm, closing_hbm, out_hbm,
    field, measured, leaf, factors, closing, weights, onehot, outgoing, held, parts, result,
    in_sem, chunk_sem, send_sem, recv_sem, out_sem, turn_sem,
):
    chunks, half, width = outgoing.shape[1:]
    slots = half // 2
    full = 2 * half
    f32, bf16 = jnp.float32, jnp.bfloat16
    grp, dev = lax.axis_index("grp"), lax.axis_index("dev")

    def bit_of(level):
        if level < 2:
            return (grp // (2 >> level)) % 2
        return (dev // (1 << (level - 2) % dev_bits)) % 2

    bits = [bit_of(level) for level in range(LEVELS)]

    def partner(level):
        turn = 1 - 2 * bits[level]
        if level < 2:
            return (grp + turn * (2 >> level), dev)
        return (grp, dev + turn * (1 << (level - 2) % dev_bits))

    def columns(chunk):
        return pl.ds(pl.multiple_of(chunk * width, width), width)

    def remote(level, chunk):
        return pltpu.make_async_remote_copy(
            src_ref=outgoing.at[level, chunk],
            dst_ref=held.at[level, chunk, pl.ds(half, half)],
            send_sem=send_sem.at[level, chunk],
            recv_sem=recv_sem.at[level, chunk],
            device_id=partner(level),
            device_id_type=MESH,
        )

    def fetch_field(chunk):
        return pltpu.make_async_copy(
            field_hbm.at[0, :, :, columns(chunk)], field.at[:, :, columns(chunk)], chunk_sem.at[chunk]
        )

    def put_result(chunk):
        return pltpu.make_async_copy(
            result.at[chunk], out_hbm.at[0, :, :, columns(chunk)], out_sem.at[chunk]
        )

    barrier = pltpu.get_barrier_semaphore()
    for level in range(LEVELS):
        pl.semaphore_signal(barrier, inc=1, device_id=partner(level), device_id_type=MESH)

    fetch_leaf = pltpu.make_async_copy(leaf_hbm.at[0], leaf, in_sem.at[0])
    fetch_leaf.start()
    for chunk in range(chunks):
        fetch_field(chunk).start()
    fetch_factors = pltpu.make_async_copy(factors_hbm.at[:, 0], factors, in_sem.at[1])
    fetch_factors.start()
    fetch_closing = pltpu.make_async_copy(closing_hbm.at[0], closing, in_sem.at[2])
    fetch_closing.start()
    fetch_measured = pltpu.make_async_copy(measured_hbm.at[0], measured, in_sem.at[3])
    fetch_measured.start()

    def store_weights(which, row, left, right):
        rows = left.shape[0]
        for side, block in ((0, left), (half, right)):
            high = block.astype(bf16)
            low = (block - high.astype(f32)).astype(bf16)
            weights[which, row : row + rows, side : side + half] = high
            weights[which, full + row : full + row + rows, side : side + half] = low

    def prepare(which, load, in_bit, out_bit):
        if out_bit is None:
            blocks = [(0, half, 0, half)]
        else:
            blocks = [
                (0, slots, (1 - out_bit) * slots, slots),
                (half, half + slots, out_bit * slots, slots),
            ]
        for real_row, imag_row, start, rows in blocks:
            if not isinstance(start, int):
                start = pl.multiple_of(start, slots)
            real = load(0, pl.ds(start, rows))
            imag = load(1, pl.ds(start, rows))
            if in_bit is None:
                store_weights(which, real_row, real, -imag)
                store_weights(which, imag_row, imag, real)
            else:
                first = lax.broadcasted_iota(jnp.int32, real.shape, 1) < slots
                real_over, imag_over = pltpu.roll(real, slots, 1), pltpu.roll(imag, slots, 1)
                own_first = in_bit == 0
                real, real_over = jnp.where(own_first, real, real_over), jnp.where(own_first, real_over, real)
                imag, imag_over = jnp.where(own_first, imag, imag_over), jnp.where(own_first, imag_over, imag)
                store_weights(
                    which, real_row, jnp.where(first, real, -imag_over), jnp.where(first, real_over, -imag)
                )
                store_weights(
                    which, imag_row, jnp.where(first, imag, real_over), jnp.where(first, imag_over, real)
                )

    def product(which, vectors):
        high = vectors.astype(bf16)
        low = (vectors - high.astype(f32)).astype(bf16)
        both = jnp.dot(weights[which], high, preferred_element_type=f32)
        rest = jnp.dot(weights[which, :full], low, preferred_element_type=f32)
        return both[:full] + (both[full:] + rest)

    def hand_on(level, chunk, coeffs):
        outgoing[level, chunk] = coeffs[:half]
        held[level, chunk, :half] = coeffs[half:]

    fetch_leaf.wait()
    prepare(0, lambda part, rows: leaf[part, rows, :], None, bits[0])
    pl.semaphore_wait(barrier, LEVELS)

    def open_chunk(chunk, carry):
        fetch_field(chunk).wait()
        vectors = field[:, :, columns(chunk)].reshape(full, width)
        hand_on(0, chunk, product(0, vectors))
        remote(0, chunk).start()
        return carry

    lax.fori_loop(0, chunks, open_chunk, 0)

    fetch_factors.wait()
    fetch_closing.wait()
    for level in range(LEVELS):
        pick = order_ref[level]
        prepare(
            1 + level,
            lambda part, rows, pick=pick: factors[pick, part, rows, :],
            bits[level],
            bits[level + 1] if level + 1 < LEVELS else None,
        )
    prepare(1 + LEVELS, lambda part, rows: closing[part, rows, :], None, None)

    def fill_onehot(step, carry):
        chunk, block = step // chunks, step % chunks
        wanted = perm_ref[:, columns(chunk)]
        source = lax.broadcasted_iota(jnp.int32, (width, width), 0) + block * width
        onehot[chunk, columns(block), :] = jnp.where(source == wanted, 1.0, 0.0).astype(bf16)
        return carry

    lax.fori_loop(0, chunks * chunks, fill_onehot, 0)
    fetch_measured.wait()

    def arrive(level, chunk):
        remote(level, chunk).wait_recv()
        return product(1 + level, held[level, chunk])

    def when_in_range(chunk, body):
        pl.when(jnp.logical_and(chunk >= 0, chunk < chunks))(lambda: body(chunk))

    def level_0(chunk):
        hand_on(1, chunk, arrive(0, chunk))
        remote(1, chunk).start()

    def level_1(chunk):
        hand_on(2, chunk, arrive(1, chunk))

    def level_2(chunk):
        hand_on(3, chunk, arrive(2, chunk))
        remote(3, chunk).start()

    def level_3(chunk):
        coeffs = arrive(3, chunk)
        high = coeffs.astype(bf16)
        parts[:full, columns(chunk)] = high
        parts[full:, columns(chunk)] = (coeffs - high.astype(f32)).astype(bf16)

    def switch(chunk):
        both = jnp.dot(parts[...], onehot[chunk], preferred_element_type=f32)
        hand_on(4, chunk, both[:full] + both[full:])
        remote(4, chunk).start()

    def middle(level, chunk):
        hand_on(level + 1, chunk, arrive(level, chunk))
        remote(level + 1, chunk).start()

    def level_7(chunk):
        image = product(1 + LEVELS, arrive(7, chunk))
        real, imag = image[:half], image[half:]
        scale = measured[:, columns(chunk)] * lax.rsqrt(jnp.maximum(real * real + imag * imag, 0.25))
        result[chunk, 0] = real * scale
        result[chunk, 1] = imag * scale
        put_result(chunk).start()

    def near(step, carry):
        when_in_range(step, level_0)
        when_in_range(step - 1, level_1)
        return carry

    lax.fori_loop(0, chunks + 1, near, 0)

    first_core = grp % 2 == 0

    @pl.when(jnp.logical_not(first_core))
    def _():
        pl.semaphore_wait(turn_sem, 1)

    for chunk in range(AHEAD):
        remote(2, chunk).start()

    def along(step, carry):
        def send_more(chunk):
            remote(2, chunk).start()

        when_in_range(step, level_2)

        @pl.when(jnp.logical_and(first_core, step == chunks - 1))
        def _():
            pl.semaphore_signal(turn_sem, inc=1, device_id=partner(1), device_id_type=MESH)

        pl.when(step + AHEAD < chunks)(lambda: send_more(step + AHEAD))
        when_in_range(step - LAG_A, level_3)
        return carry

    lax.fori_loop(0, chunks + LAG_A, along, 0)

    def across(step, carry):
        when_in_range(step, switch)
        when_in_range(step - LAG_B, functools.partial(middle, 4))
        when_in_range(step - 2 * LAG_B, functools.partial(middle, 5))
        when_in_range(step - 3 * LAG_B, functools.partial(middle, 6))
        when_in_range(step - 4 * LAG_B, level_7)
        return carry

    lax.fori_loop(0, chunks + 4 * LAG_B, across, 0)

    def finish(chunk, carry):
        put_result(chunk).wait()
        for level in range(LEVELS):
            remote(level, chunk).wait_send()
        return carry

    lax.fori_loop(0, chunks, finish, 0)


def solution(mesh):
    dev_bits = mesh.shape["dev"].bit_length() - 1

    def per_device(wavefield, measured, leaf_map, factors, closing, box_perm, factor_order):
        _, _, half, boxes = wavefield.shape
        width = min(WIDTH, boxes)
        chunks = boxes // width
        full = 2 * half
        f32, bf16 = jnp.float32, jnp.bfloat16
        anywhere = pl.BlockSpec(memory_space=pl.ANY)
        return pl.pallas_call(
            functools.partial(kernel, dev_bits),
            out_shape=jax.ShapeDtypeStruct(wavefield.shape, f32),
            in_specs=[
                pl.BlockSpec(memory_space=pltpu.SMEM),
                pl.BlockSpec(memory_space=pltpu.VMEM),
            ]
            + [anywhere] * 5,
            out_specs=anywhere,
            scratch_shapes=[
                pltpu.VMEM((2, half, boxes), f32),
                pltpu.VMEM((half, boxes), f32),
                pltpu.VMEM((2, half, half), f32),
                pltpu.VMEM((LEVELS, 2, half, half), f32),
                pltpu.VMEM((2, half, half), f32),
                pltpu.VMEM((LEVELS + 2, 2 * full, full), bf16),
                pltpu.VMEM((chunks, boxes, width), bf16),
                pltpu.VMEM((LEVELS, chunks, half, width), f32),
                pltpu.VMEM((LEVELS, chunks, full, width), f32),
                pltpu.VMEM((2 * full, boxes), bf16),
                pltpu.VMEM((chunks, 2, half, width), f32),
                pltpu.SemaphoreType.DMA((4,)),
                pltpu.SemaphoreType.DMA((chunks,)),
                pltpu.SemaphoreType.DMA((LEVELS, chunks)),
                pltpu.SemaphoreType.DMA((LEVELS, chunks)),
                pltpu.SemaphoreType.DMA((chunks,)),
                pltpu.SemaphoreType.REGULAR,
            ],
            compiler_params=pltpu.CompilerParams(
                collective_id=0, has_side_effects=True, vmem_limit_bytes=60 * 2**20
            ),
        )(factor_order, box_perm, wavefield, measured, leaf_map, factors, closing)

    return jax.shard_map(
        per_device,
        mesh=mesh,
        in_specs=(
            P(("grp", "dev"), None, None, None),
            P(("grp", "dev"), None, None),
            P(("grp", "dev"), None, None, None),
            P(None, ("grp", "dev"), None, None, None),
            P(("grp", "dev"), None, None, None),
            P(("grp", "dev"), None),
            P(),
        ),
        out_specs=P(("grp", "dev"), None, None, None),
        check_vma=False,
    )
```

```python
import functools

import jax
import jax.numpy as jnp
from jax import lax
from jax.experimental import pallas as pl
from jax.experimental.pallas import tpu as pltpu
from jax.sharding import PartitionSpec as P

MESH = pl.DeviceIdType.MESH
LEVELS = 8
VMEM_BYTES = 67043328
SWITCH = LEVELS // 2
WIDTH = 256
WIDTH_B = 128
EARLY = 4
AHEAD = 3
SPARE = 1
BEFORE = 0
LAG_2 = 3
LAG_3 = 2
LAG_4 = 3
LAG_5 = 3
LAG_6 = 3
LAG_7 = 3


def kernel(
    dev_bits, order_ref, perm_ref, field_hbm, leaf_hbm, factors_hbm, closing_hbm, image_hbm,
    field, leaf, factors, closing, weights, onehot, near_out, near_held, far_out, far_held, parts, image,
    in_sem, chunk_sem, near_send, near_recv, far_send, far_recv, out_sem, turn_sem,
):
    chunks, half, width = near_out.shape[1:]
    chunks_b, _, width_b = far_out.shape[1:]
    slots = half // 2
    full = 2 * half
    f32, bf16 = jnp.float32, jnp.bfloat16
    grp, dev = lax.axis_index("grp"), lax.axis_index("dev")

    def bit_of(level):
        if level < 2:
            return (grp // (2 >> level)) % 2
        return (dev // (1 << (level - 2) % dev_bits)) % 2

    bits = [bit_of(level) for level in range(LEVELS)]

    def partner(level):
        turn = 1 - 2 * bits[level]
        if level < 2:
            return (grp + turn * (2 >> level), dev)
        return (grp, dev + turn * (1 << (level - 2) % dev_bits))

    def columns(chunk, width=width):
        return pl.ds(pl.multiple_of(chunk * width, width), width)

    def stage(level):
        if level < SWITCH:
            return near_out.at[level], near_held.at[level], near_send.at[level], near_recv.at[level]
        level -= SWITCH
        return far_out.at[level], far_held.at[level], far_send.at[level], far_recv.at[level]

    def remote(level, chunk):
        outgoing, held, send_sem, recv_sem = stage(level)
        return pltpu.make_async_remote_copy(
            src_ref=outgoing.at[chunk],
            dst_ref=held.at[chunk, pl.ds(half, half)],
            send_sem=send_sem.at[chunk],
            recv_sem=recv_sem.at[chunk],
            device_id=partner(level),
            device_id_type=MESH,
        )

    def fetch_field(chunk):
        return pltpu.make_async_copy(
            field_hbm.at[0, :, :, columns(chunk)], field.at[:, :, columns(chunk)], chunk_sem.at[chunk]
        )

    def put_image(chunk):
        return pltpu.make_async_copy(
            image.at[chunk], image_hbm.at[0, :, :, columns(chunk, width_b)], out_sem.at[chunk]
        )

    barrier = pltpu.get_barrier_semaphore()
    for level in range(LEVELS):
        pl.semaphore_signal(barrier, inc=1, device_id=partner(level), device_id_type=MESH)

    fetch_leaf = pltpu.make_async_copy(leaf_hbm.at[0], leaf, in_sem.at[0])
    fetch_leaf.start()
    for chunk in range(chunks):
        fetch_field(chunk).start()
    fetch_factors = pltpu.make_async_copy(factors_hbm.at[:, 0], factors, in_sem.at[1])
    fetch_factors.start()
    fetch_closing = pltpu.make_async_copy(closing_hbm.at[0], closing, in_sem.at[2])
    fetch_closing.start()

    def store_weights(which, row, left, right):
        rows = left.shape[0]
        for side, block in ((0, left), (half, right)):
            high = block.astype(bf16)
            low = (block - high.astype(f32)).astype(bf16)
            weights[which, row : row + rows, side : side + half] = high
            weights[which, full + row : full + row + rows, side : side + half] = low

    def prepare(which, load, in_bit, out_bit):
        if out_bit is None:
            blocks = [(0, half, 0, half)]
        else:
            blocks = [
                (0, slots, (1 - out_bit) * slots, slots),
                (half, half + slots, out_bit * slots, slots),
            ]
        for real_row, imag_row, start, rows in blocks:
            if not isinstance(start, int):
                start = pl.multiple_of(start, slots)
            real = load(0, pl.ds(start, rows))
            imag = load(1, pl.ds(start, rows))
            if in_bit is None:
                store_weights(which, real_row, real, -imag)
                store_weights(which, imag_row, imag, real)
            else:
                first = lax.broadcasted_iota(jnp.int32, real.shape, 1) < slots
                real_over, imag_over = pltpu.roll(real, slots, 1), pltpu.roll(imag, slots, 1)
                own_first = in_bit == 0
                real, real_over = jnp.where(own_first, real, real_over), jnp.where(own_first, real_over, real)
                imag, imag_over = jnp.where(own_first, imag, imag_over), jnp.where(own_first, imag_over, imag)
                store_weights(
                    which, real_row, jnp.where(first, real, -imag_over), jnp.where(first, real_over, -imag)
                )
                store_weights(
                    which, imag_row, jnp.where(first, imag, real_over), jnp.where(first, imag_over, real)
                )

    def product(which, vectors):
        high = vectors.astype(bf16)
        low = (vectors - high.astype(f32)).astype(bf16)
        both = jnp.dot(weights[which], high, preferred_element_type=f32)
        rest = jnp.dot(weights[which, :full], low, preferred_element_type=f32)
        return both[:full] + (both[full:] + rest)

    def hand_on(level, chunk, coeffs):
        outgoing, held, _, _ = stage(level)
        outgoing[chunk] = coeffs[:half]
        held[chunk, :half] = coeffs[half:]

    fetch_leaf.wait()
    prepare(0, lambda part, rows: leaf[part, rows, :], None, bits[0])
    pl.semaphore_wait(barrier, LEVELS)

    def open_chunk(chunk, carry):
        fetch_field(chunk).wait()
        vectors = field[:, :, columns(chunk)].reshape(full, width)
        hand_on(0, chunk, product(0, vectors))
        pl.when(chunk < EARLY)(lambda: remote(0, chunk).start())
        return carry

    lax.fori_loop(0, chunks, open_chunk, 0)

    fetch_factors.wait()
    fetch_closing.wait()
    for level in range(LEVELS):
        pick = order_ref[level]
        prepare(
            1 + level,
            lambda part, rows, pick=pick: factors[pick, part, rows, :],
            bits[level],
            bits[level + 1] if level + 1 < LEVELS else None,
        )
    prepare(0, lambda part, rows: closing[part, rows, :], None, None)
    last = weights[LEVELS, :full].astype(f32) + weights[LEVELS, full:].astype(f32)
    last = product(0, last)
    high = last.astype(bf16)
    weights[LEVELS, :full] = high
    weights[LEVELS, full:] = (last - high.astype(f32)).astype(bf16)

    def fill_onehot(step, carry):
        chunk, block = step // chunks, step % chunks
        wanted = perm_ref[:, columns(chunk)]
        source = lax.broadcasted_iota(jnp.int32, (width, width), 0) + block * width
        onehot[chunk, columns(block), :] = jnp.where(source == wanted, 1.0, 0.0).astype(bf16)
        return carry

    lax.fori_loop(0, chunks * chunks, fill_onehot, 0)

    def clear(chunk, carry):
        hand_on(SWITCH, chunk, jnp.zeros((full, width_b), f32))
        return carry

    lax.fori_loop(0, chunks_b, clear, 0)

    def arrive(level, chunk):
        remote(level, chunk).wait_recv()
        return product(1 + level, stage(level)[1][chunk])

    def when_in_range(chunk, body, chunks=chunks):
        pl.when(jnp.logical_and(chunk >= 0, chunk < chunks))(lambda: body(chunk))

    def level_0(chunk):
        hand_on(1, chunk, arrive(0, chunk))
        remote(1, chunk).start()

    def level_1(chunk):
        hand_on(2, chunk, arrive(1, chunk))

    def level_2(chunk):
        hand_on(3, chunk, arrive(2, chunk))
        remote(3, chunk).start()

    def level_3(chunk):
        coeffs = arrive(3, chunk)
        high = coeffs.astype(bf16)
        parts[:full] = high
        parts[full:] = (coeffs - high.astype(f32)).astype(bf16)

        def place(target, carry):
            both = jnp.dot(parts[...], onehot[target, columns(chunk), :], preferred_element_type=f32)
            both = both[:full] + both[full:]
            for piece in range(width // width_b):
                which = target * (width // width_b) + piece
                block = both[:, piece * width_b : (piece + 1) * width_b]
                far_out[0, which] += block[:half]
                far_held[0, which, :half] += block[half:]
            return carry

        lax.fori_loop(0, chunks, place, 0, unroll=2)

    def switch(chunk):
        remote(SWITCH, chunk).start()

    def middle(level, chunk):
        hand_on(level + 1, chunk, arrive(level, chunk))
        remote(level + 1, chunk).start()

    def level_7(chunk):
        coeffs = arrive(7, chunk)
        image[chunk, 0] = coeffs[:half]
        image[chunk, 1] = coeffs[half:]
        put_image(chunk).start()

    first_core = grp % 2 == 0

    def send(level, chunk):
        remote(level, chunk).start()

    def near(step, carry):
        when_in_range(step, level_0)
        pl.when(step + EARLY < chunks)(lambda: send(0, step + EARLY))
        when_in_range(step - 1, level_1)
        return carry

    def along(step, carry):
        when_in_range(step, level_2)

        @pl.when(jnp.logical_and(first_core, step == chunks - SPARE))
        def _():
            pl.semaphore_signal(turn_sem, inc=1, device_id=partner(1), device_id_type=MESH)

        when_in_range(step - LAG_3, level_3)
        return carry

    @pl.when(first_core)
    def _():
        def both(step, carry):
            near(step, carry)
            when_in_range(step - 1, functools.partial(send, 2))
            return along(step - LAG_2, carry)

        lax.fori_loop(0, chunks + LAG_2 + LAG_3, both, 0)

    @pl.when(jnp.logical_not(first_core))
    def _():
        def open_turn():
            for chunk in range(AHEAD):
                send(2, chunk)

        lax.fori_loop(0, chunks + 1, near, 0)
        if BEFORE:
            open_turn()
        pl.semaphore_wait(turn_sem, 1)
        if not BEFORE:
            open_turn()

        def rest(step, carry):
            along(step, carry)
            pl.when(step + AHEAD < chunks)(lambda: send(2, step + AHEAD))
            return carry

        lax.fori_loop(0, chunks + LAG_3, rest, 0)

    def leave(levels, chunk):
        for level in levels:
            remote(level, chunk).wait_send()

    lags = (0, LAG_4, LAG_4 + LAG_5, LAG_4 + LAG_5 + LAG_6, LAG_4 + LAG_5 + LAG_6 + LAG_7)

    def across(step, carry):
        when_in_range(step, switch, chunks_b)
        when_in_range(step - lags[1], functools.partial(middle, 4), chunks_b)
        when_in_range(step - lags[2], functools.partial(middle, 5), chunks_b)
        when_in_range(step - lags[3], functools.partial(middle, 6), chunks_b)
        when_in_range(step - lags[4], level_7, chunks_b)
        when_in_range(step, functools.partial(leave, range(SWITCH)))
        when_in_range(step - lags[4], functools.partial(leave, range(SWITCH, LEVELS)), chunks_b)
        return carry

    lax.fori_loop(0, chunks_b + lags[4], across, 0)

    def finish(chunk, carry):
        put_image(chunk).wait()
        return carry

    lax.fori_loop(0, chunks_b, finish, 0)


def project(image_hbm, measured_hbm, out_hbm, image, measured, in_sem, measured_sem, out_sem):
    chunks, _, _, width = image.shape

    def columns(chunk):
        return pl.ds(pl.multiple_of(chunk * width, width), width)

    def get(chunk):
        return pltpu.make_async_copy(image_hbm.at[0, :, :, columns(chunk)], image.at[chunk], in_sem.at[chunk])

    def put(chunk):
        return pltpu.make_async_copy(image.at[chunk], out_hbm.at[0, :, :, columns(chunk)], out_sem.at[chunk])

    def get_measured(chunk):
        return pltpu.make_async_copy(
            measured_hbm.at[0, :, columns(chunk)], measured.at[chunk], measured_sem.at[chunk]
        )

    for chunk in range(chunks):
        get(chunk).start()
        get_measured(chunk).start()

    def step(chunk, carry):
        get(chunk).wait()
        get_measured(chunk).wait()
        real, imag = image[chunk, 0], image[chunk, 1]
        scale = measured[chunk] * lax.rsqrt(jnp.maximum(real * real + imag * imag, 0.25))
        image[chunk, 0] = real * scale
        image[chunk, 1] = imag * scale
        put(chunk).start()
        return carry

    def finish(chunk, carry):
        put(chunk).wait()
        return carry

    lax.fori_loop(0, chunks, step, 0)
    lax.fori_loop(0, chunks, finish, 0)


def solution(mesh):
    dev_bits = mesh.shape["dev"].bit_length() - 1

    def per_device(wavefield, measured, leaf_map, factors, closing, box_perm, factor_order):
        _, _, half, boxes = wavefield.shape
        width, width_b = min(WIDTH, boxes), min(WIDTH_B, boxes)
        chunks, chunks_b = boxes // width, boxes // width_b
        full = 2 * half
        f32, bf16 = jnp.float32, jnp.bfloat16
        in_hbm = pl.BlockSpec(memory_space=pltpu.HBM)
        in_vmem = pl.BlockSpec(memory_space=pltpu.VMEM)
        image = pl.pallas_call(
            functools.partial(kernel, dev_bits),
            out_shape=jax.ShapeDtypeStruct(wavefield.shape, f32),
            in_specs=[
                pl.BlockSpec(memory_space=pltpu.SMEM),
                in_vmem,
            ]
            + [in_hbm] * 4,
            out_specs=in_hbm,
            scratch_shapes=[
                pltpu.VMEM((2, half, boxes), f32),
                pltpu.VMEM((2, half, half), f32),
                pltpu.VMEM((LEVELS, 2, half, half), f32),
                pltpu.VMEM((2, half, half), f32),
                pltpu.VMEM((LEVELS + 1, 2 * full, full), bf16),
                pltpu.VMEM((chunks, boxes, width), bf16),
                pltpu.VMEM((SWITCH, chunks, half, width), f32),
                pltpu.VMEM((SWITCH, chunks, full, width), f32),
                pltpu.VMEM((LEVELS - SWITCH, chunks_b, half, width_b), f32),
                pltpu.VMEM((LEVELS - SWITCH, chunks_b, full, width_b), f32),
                pltpu.VMEM((2 * full, width), bf16),
                pltpu.VMEM((chunks_b, 2, half, width_b), f32),
                pltpu.SemaphoreType.DMA((3,)),
                pltpu.SemaphoreType.DMA((chunks,)),
                pltpu.SemaphoreType.DMA((SWITCH, chunks)),
                pltpu.SemaphoreType.DMA((SWITCH, chunks)),
                pltpu.SemaphoreType.DMA((LEVELS - SWITCH, chunks_b)),
                pltpu.SemaphoreType.DMA((LEVELS - SWITCH, chunks_b)),
                pltpu.SemaphoreType.DMA((chunks_b,)),
                pltpu.SemaphoreType.REGULAR,
            ],
            compiler_params=pltpu.CompilerParams(
                collective_id=0, has_side_effects=True, vmem_limit_bytes=VMEM_BYTES
            ),
        )(factor_order, box_perm, wavefield, leaf_map, factors, closing)
        return pl.pallas_call(
            project,
            out_shape=jax.ShapeDtypeStruct(wavefield.shape, f32),
            in_specs=[in_hbm, in_hbm],
            out_specs=in_hbm,
            scratch_shapes=[
                pltpu.VMEM((chunks, 2, half, width), f32),
                pltpu.VMEM((chunks, half, width), f32),
                pltpu.SemaphoreType.DMA((chunks,)),
                pltpu.SemaphoreType.DMA((chunks,)),
                pltpu.SemaphoreType.DMA((chunks,)),
            ],
            compiler_params=pltpu.CompilerParams(vmem_limit_bytes=VMEM_BYTES),
        )(image, measured)

    return jax.shard_map(
        per_device,
        mesh=mesh,
        in_specs=(
            P(("grp", "dev"), None, None, None),
            P(("grp", "dev"), None, None),
            P(("grp", "dev"), None, None, None),
            P(None, ("grp", "dev"), None, None, None),
            P(("grp", "dev"), None, None, None),
            P(("grp", "dev"), None),
            P(),
        ),
        out_specs=P(("grp", "dev"), None, None, None),
        check_vma=False,
    )
```

```python
import functools

import jax
import jax.numpy as jnp
from jax import lax
from jax.experimental import pallas as pl
from jax.experimental.pallas import tpu as pltpu
from jax.sharding import PartitionSpec as P

MESH = pl.DeviceIdType.MESH
LEVELS = 8
VMEM_BYTES = 67043328
SWITCH = LEVELS // 2
WIDTH = 256
WIDTH_B = 128
EARLY = 5
AHEAD = 3
SPARE = 1
BEFORE = 0
LAG_2 = 3
LAG_3 = 3
ROWS = 16
FIRST = 2
UNROLL = 2
LAG_4 = 3
LAG_5 = 3
LAG_6 = 2
LAG_7 = 3


def kernel(
    dev_bits, order_ref, perm_ref, field_hbm, leaf_hbm, factors_hbm, closing_hbm, image_hbm,
    field, leaf, factors, closing, weights, onehot, near_out, near_held, far_out, far_held, parts, image,
    in_sem, chunk_sem, near_send, near_recv, far_send, far_recv, out_sem, turn_sem,
):
    chunks, half, width = near_out.shape[1:]
    chunks_b, _, width_b = far_out.shape[1:]
    pieces = width // width_b
    slots = half // 2
    full = 2 * half
    f32, bf16 = jnp.float32, jnp.bfloat16
    grp, dev = lax.axis_index("grp"), lax.axis_index("dev")

    def bit_of(level):
        if level < 2:
            return (grp // (2 >> level)) % 2
        return (dev // (1 << (level - 2) % dev_bits)) % 2

    bits = [bit_of(level) for level in range(LEVELS)]

    def partner(level):
        turn = 1 - 2 * bits[level]
        if level < 2:
            return (grp + turn * (2 >> level), dev)
        return (grp, dev + turn * (1 << (level - 2) % dev_bits))

    def columns(chunk, width=width):
        return pl.ds(pl.multiple_of(chunk * width, width), width)

    def stage(level):
        if level < SWITCH:
            return near_out.at[level], near_held.at[level], near_send.at[level], near_recv.at[level]
        level -= SWITCH
        return far_out.at[level], far_held.at[level], far_send.at[level], far_recv.at[level]

    def remote(level, chunk):
        outgoing, held, send_sem, recv_sem = stage(level)
        return pltpu.make_async_remote_copy(
            src_ref=outgoing.at[chunk],
            dst_ref=held.at[chunk, pl.ds(half, half)],
            send_sem=send_sem.at[chunk],
            recv_sem=recv_sem.at[chunk],
            device_id=partner(level),
            device_id_type=MESH,
        )

    def fetch_field(chunk):
        return pltpu.make_async_copy(
            field_hbm.at[0, :, :, columns(chunk)], field.at[:, :, columns(chunk)], chunk_sem.at[chunk]
        )

    def put_image(chunk):
        return pltpu.make_async_copy(
            image.at[chunk], image_hbm.at[0, :, :, columns(chunk, width_b)], out_sem.at[chunk]
        )

    barrier = pltpu.get_barrier_semaphore()
    for level in range(LEVELS):
        pl.semaphore_signal(barrier, inc=1, device_id=partner(level), device_id_type=MESH)

    fetch_leaf = pltpu.make_async_copy(leaf_hbm.at[0], leaf, in_sem.at[0])
    fetch_leaf.start()
    for chunk in range(chunks):
        fetch_field(chunk).start()
    fetch_factors = pltpu.make_async_copy(factors_hbm.at[:, 0], factors, in_sem.at[1])
    fetch_factors.start()
    fetch_closing = pltpu.make_async_copy(closing_hbm.at[0], closing, in_sem.at[2])
    fetch_closing.start()

    def store_weights(which, row, left, right):
        rows = left.shape[0]
        for side, block in ((0, left), (half, right)):
            high = block.astype(bf16)
            low = (block - high.astype(f32)).astype(bf16)
            weights[which, row : row + rows, side : side + half] = high
            weights[which, full + row : full + row + rows, side : side + half] = low

    def prepare(which, load, in_bit, out_bit):
        if out_bit is None:
            blocks = [(0, half, 0, half)]
        else:
            blocks = [
                (0, slots, (1 - out_bit) * slots, slots),
                (half, half + slots, out_bit * slots, slots),
            ]
        for real_row, imag_row, start, rows in blocks:
            if not isinstance(start, int):
                start = pl.multiple_of(start, slots)
            real = load(0, pl.ds(start, rows))
            imag = load(1, pl.ds(start, rows))
            if in_bit is None:
                store_weights(which, real_row, real, -imag)
                store_weights(which, imag_row, imag, real)
            else:
                first = lax.broadcasted_iota(jnp.int32, real.shape, 1) < slots
                real_over, imag_over = pltpu.roll(real, slots, 1), pltpu.roll(imag, slots, 1)
                own_first = in_bit == 0
                real, real_over = jnp.where(own_first, real, real_over), jnp.where(own_first, real_over, real)
                imag, imag_over = jnp.where(own_first, imag, imag_over), jnp.where(own_first, imag_over, imag)
                store_weights(
                    which, real_row, jnp.where(first, real, -imag_over), jnp.where(first, real_over, -imag)
                )
                store_weights(
                    which, imag_row, jnp.where(first, imag, real_over), jnp.where(first, imag_over, real)
                )

    def product(which, vectors):
        high = vectors.astype(bf16)
        low = (vectors - high.astype(f32)).astype(bf16)
        both = jnp.dot(weights[which], high, preferred_element_type=f32)
        rest = jnp.dot(weights[which, :full], low, preferred_element_type=f32)
        return both[:full] + (both[full:] + rest)

    def hand_on(level, chunk, coeffs):
        outgoing, held, _, _ = stage(level)
        outgoing[chunk] = coeffs[:half]
        held[chunk, :half] = coeffs[half:]

    fetch_leaf.wait()
    prepare(0, lambda part, rows: leaf[part, rows, :], None, bits[0])
    pl.semaphore_wait(barrier, LEVELS)

    def open_chunk(chunk, carry):
        fetch_field(chunk).wait()
        vectors = field[:, :, columns(chunk)].reshape(full, width)
        hand_on(0, chunk, product(0, vectors))
        pl.when(chunk < EARLY)(lambda: remote(0, chunk).start())
        return carry

    lax.fori_loop(0, chunks, open_chunk, 0)

    fetch_factors.wait()
    fetch_closing.wait()
    for level in range(LEVELS):
        pick = order_ref[level]
        prepare(
            1 + level,
            lambda part, rows, pick=pick: factors[pick, part, rows, :],
            bits[level],
            bits[level + 1] if level + 1 < LEVELS else None,
        )
    prepare(0, lambda part, rows: closing[part, rows, :], None, None)
    last = weights[LEVELS, :full].astype(f32) + weights[LEVELS, full:].astype(f32)
    last = product(0, last)
    high = last.astype(bf16)
    weights[LEVELS, :full] = high
    weights[LEVELS, full:] = (last - high.astype(f32)).astype(bf16)

    def fill_onehot(step, carry):
        chunk, block = step // chunks, step % chunks
        wanted = perm_ref[:, columns(chunk)]
        source = lax.broadcasted_iota(jnp.int32, (width, width), 0) + block * width
        onehot[chunk, columns(block), :] = jnp.where(source == wanted, 1.0, 0.0).astype(bf16)
        return carry

    lax.fori_loop(0, chunks * chunks, fill_onehot, 0)

    def clear(chunk, carry):
        hand_on(SWITCH, chunk, jnp.zeros((full, width_b), f32))
        return carry

    lax.fori_loop(0, chunks_b, clear, 0)

    def arrive(level, chunk):
        remote(level, chunk).wait_recv()
        return product(1 + level, stage(level)[1][chunk])

    def when_in_range(chunk, body, chunks=chunks):
        pl.when(jnp.logical_and(chunk >= 0, chunk < chunks))(lambda: body(chunk))

    def level_0(chunk):
        hand_on(1, chunk, arrive(0, chunk))
        remote(1, chunk).start()

    def level_1(chunk):
        hand_on(2, chunk, arrive(1, chunk))

    def level_2(chunk):
        hand_on(3, chunk, arrive(2, chunk))
        remote(3, chunk).start()

    def take(chunk):
        coeffs = arrive(3, chunk)
        high = coeffs.astype(bf16)
        parts[:full] = high
        parts[full:] = (coeffs - high.astype(f32)).astype(bf16)

    def place(chunk, target):
        both = jnp.dot(parts[...], onehot[target, columns(chunk), :], preferred_element_type=f32)
        both = both[:full] + both[full:]
        for piece in range(pieces):
            which = target * pieces + piece
            block = both[:, piece * width_b : (piece + 1) * width_b]
            far_out[0, which] += block[:half]
            far_held[0, which, :half] += block[half:]

    def place_from(chunk, first):
        def one(target, carry):
            place(chunk, target)
            return carry

        lax.fori_loop(first, chunks, one, 0, unroll=UNROLL)

    def level_3(chunk):
        take(chunk)
        place_from(chunk, 0)

    def last_level_3():
        take(chunks - 1)
        for target in range(FIRST):
            place(chunks - 1, target)
            for piece in range(pieces):
                remote(SWITCH, target * pieces + piece).start()
        place_from(chunks - 1, FIRST)

    def switch(chunk):
        pl.when(chunk >= FIRST * pieces)(lambda: remote(SWITCH, chunk).start())

    def middle(level, chunk):
        hand_on(level + 1, chunk, arrive(level, chunk))
        remote(level + 1, chunk).start()

    def level_7(chunk):
        coeffs = arrive(7, chunk)
        image[chunk, 0] = coeffs[:half]
        image[chunk, 1] = coeffs[half:]
        put_image(chunk).start()

    first_core = grp % 2 == 0

    def send(level, chunk):
        remote(level, chunk).start()

    def near(step, carry):
        when_in_range(step, level_0)
        pl.when(step + EARLY < chunks)(lambda: send(0, step + EARLY))
        when_in_range(step - 1, level_1)
        return carry

    def along(step, carry):
        when_in_range(step, level_2)

        @pl.when(jnp.logical_and(first_core, step == chunks - SPARE))
        def _():
            pl.semaphore_signal(turn_sem, inc=1, device_id=partner(1), device_id_type=MESH)

        when_in_range(step - LAG_3, level_3, chunks - 1)
        return carry

    @pl.when(first_core)
    def _():
        def both(step, carry):
            near(step, carry)
            when_in_range(step - 1, functools.partial(send, 2))
            return along(step - LAG_2, carry)

        lax.fori_loop(0, chunks - 1 + LAG_2 + LAG_3, both, 0)

    @pl.when(jnp.logical_not(first_core))
    def _():
        def open_turn():
            for chunk in range(AHEAD):
                send(2, chunk)

        lax.fori_loop(0, chunks + 1, near, 0)
        if BEFORE:
            open_turn()
        pl.semaphore_wait(turn_sem, 1)
        if not BEFORE:
            open_turn()

        def rest(step, carry):
            along(step, carry)
            pl.when(step + AHEAD < chunks)(lambda: send(2, step + AHEAD))
            return carry

        lax.fori_loop(0, chunks - 1 + LAG_3, rest, 0)

    last_level_3()

    def leave(levels, chunk):
        for level in levels:
            remote(level, chunk).wait_send()

    lags = (0, LAG_4, LAG_4 + LAG_5, LAG_4 + LAG_5 + LAG_6, LAG_4 + LAG_5 + LAG_6 + LAG_7)

    def across(step, carry):
        when_in_range(step, switch, chunks_b)
        when_in_range(step - lags[1], functools.partial(middle, 4), chunks_b)
        when_in_range(step - lags[2], functools.partial(middle, 5), chunks_b)
        when_in_range(step - lags[3], functools.partial(middle, 6), chunks_b)
        when_in_range(step - lags[4], level_7, chunks_b)
        when_in_range(step, functools.partial(leave, range(SWITCH)))
        when_in_range(step - lags[4], functools.partial(leave, range(SWITCH, LEVELS)), chunks_b)
        return carry

    lax.fori_loop(0, chunks_b + lags[4], across, 0)

    def finish(chunk, carry):
        put_image(chunk).wait()
        return carry

    lax.fori_loop(0, chunks_b, finish, 0)


def project(image_hbm, measured_hbm, out_hbm, image, measured, in_sem, measured_sem, out_sem):
    chunks, _, rows, _ = image.shape

    def part(chunk):
        return pl.ds(pl.multiple_of(chunk * rows, rows), rows)

    def get(chunk):
        return pltpu.make_async_copy(image_hbm.at[0, :, part(chunk)], image.at[chunk], in_sem.at[chunk])

    def get_measured(chunk):
        return pltpu.make_async_copy(measured_hbm.at[0, part(chunk)], measured.at[chunk], measured_sem.at[chunk])

    def put(chunk):
        return pltpu.make_async_copy(image.at[chunk], out_hbm.at[0, :, part(chunk)], out_sem.at[chunk])

    for chunk in range(chunks):
        get(chunk).start()
        get_measured(chunk).start()

    def step(chunk, carry):
        get(chunk).wait()
        get_measured(chunk).wait()
        real, imag = image[chunk, 0], image[chunk, 1]
        scale = measured[chunk] * lax.rsqrt(jnp.maximum(real * real + imag * imag, 0.25))
        image[chunk, 0] = real * scale
        image[chunk, 1] = imag * scale
        put(chunk).start()
        return carry

    def finish(chunk, carry):
        put(chunk).wait()
        return carry

    lax.fori_loop(0, chunks, step, 0)
    lax.fori_loop(0, chunks, finish, 0)


def solution(mesh):
    dev_bits = mesh.shape["dev"].bit_length() - 1

    def per_device(wavefield, measured, leaf_map, factors, closing, box_perm, factor_order):
        _, _, half, boxes = wavefield.shape
        width, width_b = min(WIDTH, boxes), min(WIDTH_B, boxes)
        chunks, chunks_b = boxes // width, boxes // width_b
        full = 2 * half
        f32, bf16 = jnp.float32, jnp.bfloat16
        in_hbm = pl.BlockSpec(memory_space=pltpu.HBM)
        in_vmem = pl.BlockSpec(memory_space=pltpu.VMEM)
        image = pl.pallas_call(
            functools.partial(kernel, dev_bits),
            out_shape=jax.ShapeDtypeStruct(wavefield.shape, f32),
            in_specs=[
                pl.BlockSpec(memory_space=pltpu.SMEM),
                in_vmem,
            ]
            + [in_hbm] * 4,
            out_specs=in_hbm,
            scratch_shapes=[
                pltpu.VMEM((2, half, boxes), f32),
                pltpu.VMEM((2, half, half), f32),
                pltpu.VMEM((LEVELS, 2, half, half), f32),
                pltpu.VMEM((2, half, half), f32),
                pltpu.VMEM((LEVELS + 1, 2 * full, full), bf16),
                pltpu.VMEM((chunks, boxes, width), bf16),
                pltpu.VMEM((SWITCH, chunks, half, width), f32),
                pltpu.VMEM((SWITCH, chunks, full, width), f32),
                pltpu.VMEM((LEVELS - SWITCH, chunks_b, half, width_b), f32),
                pltpu.VMEM((LEVELS - SWITCH, chunks_b, full, width_b), f32),
                pltpu.VMEM((2 * full, width), bf16),
                pltpu.VMEM((chunks_b, 2, half, width_b), f32),
                pltpu.SemaphoreType.DMA((3,)),
                pltpu.SemaphoreType.DMA((chunks,)),
                pltpu.SemaphoreType.DMA((SWITCH, chunks)),
                pltpu.SemaphoreType.DMA((SWITCH, chunks)),
                pltpu.SemaphoreType.DMA((LEVELS - SWITCH, chunks_b)),
                pltpu.SemaphoreType.DMA((LEVELS - SWITCH, chunks_b)),
                pltpu.SemaphoreType.DMA((chunks_b,)),
                pltpu.SemaphoreType.REGULAR,
            ],
            compiler_params=pltpu.CompilerParams(
                collective_id=0, has_side_effects=True, vmem_limit_bytes=VMEM_BYTES
            ),
        )(factor_order, box_perm, wavefield, leaf_map, factors, closing)
        return pl.pallas_call(
            project,
            out_shape=jax.ShapeDtypeStruct(wavefield.shape, f32),
            in_specs=[in_hbm, in_hbm],
            out_specs=in_hbm,
            scratch_shapes=[
                pltpu.VMEM((half // ROWS, 2, ROWS, boxes), f32),
                pltpu.VMEM((half // ROWS, ROWS, boxes), f32),
                pltpu.SemaphoreType.DMA((half // ROWS,)),
                pltpu.SemaphoreType.DMA((half // ROWS,)),
                pltpu.SemaphoreType.DMA((half // ROWS,)),
            ],
            compiler_params=pltpu.CompilerParams(vmem_limit_bytes=VMEM_BYTES),
        )(image, measured)

    return jax.shard_map(
        per_device,
        mesh=mesh,
        in_specs=(
            P(("grp", "dev"), None, None, None),
            P(("grp", "dev"), None, None),
            P(("grp", "dev"), None, None, None),
            P(None, ("grp", "dev"), None, None, None),
            P(("grp", "dev"), None, None, None),
            P(("grp", "dev"), None),
            P(),
        ),
        out_specs=P(("grp", "dev"), None, None, None),
        check_vma=False,
    )
```

```python
import functools

import jax
import jax.numpy as jnp
from jax import lax
from jax.experimental import pallas as pl
from jax.experimental.pallas import tpu as pltpu
from jax.sharding import PartitionSpec as P

MESH = pl.DeviceIdType.MESH
LEVELS = 8
VMEM_BYTES = 67043328
SWITCH = LEVELS // 2
WIDTH = 256
WIDTH_B = 128
EARLY = 5
AHEAD = 3
SPARE = 1
BEFORE = 0
LAG_2 = 3
LAG_3 = 3
ROWS = 16
FIRST = 2
UNROLL = 2
LAG_4 = 3
LAG_5 = 3
LAG_6 = 2
LAG_7 = 3


def kernel(
    dev_bits, order_ref, perm_ref, field_hbm, measured_hbm, leaf_hbm, factors_hbm, closing_hbm, image_hbm,
    field, measured, leaf, factors, closing, weights, onehot, near_out, near_held, far_out, far_held, parts, image,
    in_sem, chunk_sem, near_send, near_recv, far_send, far_recv, out_sem, turn_sem,
):
    chunks, half, width = near_out.shape[1:]
    chunks_b, _, width_b = far_out.shape[1:]
    pieces = width // width_b
    slots = half // 2
    full = 2 * half
    f32, bf16 = jnp.float32, jnp.bfloat16
    grp, dev = lax.axis_index("grp"), lax.axis_index("dev")

    def bit_of(level):
        if level < 2:
            return (grp // (2 >> level)) % 2
        return (dev // (1 << (level - 2) % dev_bits)) % 2

    bits = [bit_of(level) for level in range(LEVELS)]

    def partner(level):
        turn = 1 - 2 * bits[level]
        if level < 2:
            return (grp + turn * (2 >> level), dev)
        return (grp, dev + turn * (1 << (level - 2) % dev_bits))

    def columns(chunk, width=width):
        return pl.ds(pl.multiple_of(chunk * width, width), width)

    def stage(level):
        if level < SWITCH:
            return near_out.at[level], near_held.at[level], near_send.at[level], near_recv.at[level]
        level -= SWITCH
        return far_out.at[level], far_held.at[level], far_send.at[level], far_recv.at[level]

    def remote(level, chunk):
        outgoing, held, send_sem, recv_sem = stage(level)
        return pltpu.make_async_remote_copy(
            src_ref=outgoing.at[chunk],
            dst_ref=held.at[chunk, pl.ds(half, half)],
            send_sem=send_sem.at[chunk],
            recv_sem=recv_sem.at[chunk],
            device_id=partner(level),
            device_id_type=MESH,
        )

    def fetch_field(chunk):
        return pltpu.make_async_copy(
            field_hbm.at[0, :, :, columns(chunk)], field.at[:, :, columns(chunk)], chunk_sem.at[chunk]
        )

    def put_image(chunk):
        return pltpu.make_async_copy(
            image.at[chunk], image_hbm.at[0, :, :, columns(chunk, width_b)], out_sem.at[chunk]
        )

    barrier = pltpu.get_barrier_semaphore()
    for level in range(LEVELS):
        pl.semaphore_signal(barrier, inc=1, device_id=partner(level), device_id_type=MESH)

    fetch_leaf = pltpu.make_async_copy(leaf_hbm.at[0], leaf, in_sem.at[0])
    fetch_leaf.start()
    for chunk in range(chunks):
        fetch_field(chunk).start()
    fetch_factors = pltpu.make_async_copy(factors_hbm.at[:, 0], factors, in_sem.at[1])
    fetch_factors.start()
    fetch_closing = pltpu.make_async_copy(closing_hbm.at[0], closing, in_sem.at[2])
    fetch_closing.start()
    fetch_measured = pltpu.make_async_copy(measured_hbm.at[0], measured, in_sem.at[3])
    fetch_measured.start()

    def store_weights(which, row, left, right):
        rows = left.shape[0]
        for side, block in ((0, left), (half, right)):
            high = block.astype(bf16)
            low = (block - high.astype(f32)).astype(bf16)
            weights[which, row : row + rows, side : side + half] = high
            weights[which, full + row : full + row + rows, side : side + half] = low

    def prepare(which, load, in_bit, out_bit):
        if out_bit is None:
            blocks = [(0, half, 0, half)]
        else:
            blocks = [
                (0, slots, (1 - out_bit) * slots, slots),
                (half, half + slots, out_bit * slots, slots),
            ]
        for real_row, imag_row, start, rows in blocks:
            if not isinstance(start, int):
                start = pl.multiple_of(start, slots)
            real = load(0, pl.ds(start, rows))
            imag = load(1, pl.ds(start, rows))
            if in_bit is None:
                store_weights(which, real_row, real, -imag)
                store_weights(which, imag_row, imag, real)
            else:
                first = lax.broadcasted_iota(jnp.int32, real.shape, 1) < slots
                real_over, imag_over = pltpu.roll(real, slots, 1), pltpu.roll(imag, slots, 1)
                own_first = in_bit == 0
                real, real_over = jnp.where(own_first, real, real_over), jnp.where(own_first, real_over, real)
                imag, imag_over = jnp.where(own_first, imag, imag_over), jnp.where(own_first, imag_over, imag)
                store_weights(
                    which, real_row, jnp.where(first, real, -imag_over), jnp.where(first, real_over, -imag)
                )
                store_weights(
                    which, imag_row, jnp.where(first, imag, real_over), jnp.where(first, imag_over, real)
                )

    def product(which, vectors):
        high = vectors.astype(bf16)
        low = (vectors - high.astype(f32)).astype(bf16)
        count = vectors.shape[1]
        if count <= 128:
            all_four = jnp.dot(weights[which], jnp.concatenate([high, low], axis=1), preferred_element_type=f32)
            return all_four[:full, :count] + (all_four[full:, :count] + all_four[:full, count:])
        both = jnp.dot(weights[which], high, preferred_element_type=f32)
        rest = jnp.dot(weights[which, :full], low, preferred_element_type=f32)
        return both[:full] + (both[full:] + rest)

    def hand_on(level, chunk, coeffs):
        outgoing, held, _, _ = stage(level)
        outgoing[chunk] = coeffs[:half]
        held[chunk, :half] = coeffs[half:]

    fetch_leaf.wait()
    prepare(0, lambda part, rows: leaf[part, rows, :], None, bits[0])
    pl.semaphore_wait(barrier, LEVELS)

    def open_chunk(chunk, carry):
        fetch_field(chunk).wait()
        vectors = field[:, :, columns(chunk)].reshape(full, width)
        hand_on(0, chunk, product(0, vectors))
        pl.when(chunk < EARLY)(lambda: remote(0, chunk).start())
        return carry

    lax.fori_loop(0, chunks, open_chunk, 0)

    fetch_factors.wait()
    fetch_closing.wait()
    for level in range(LEVELS):
        pick = order_ref[level]
        prepare(
            1 + level,
            lambda part, rows, pick=pick: factors[pick, part, rows, :],
            bits[level],
            bits[level + 1] if level + 1 < LEVELS else None,
        )
    prepare(0, lambda part, rows: closing[part, rows, :], None, None)
    last = weights[LEVELS, :full].astype(f32) + weights[LEVELS, full:].astype(f32)
    last = product(0, last)
    high = last.astype(bf16)
    weights[LEVELS, :full] = high
    weights[LEVELS, full:] = (last - high.astype(f32)).astype(bf16)

    def fill_onehot(step, carry):
        chunk, block = step // chunks, step % chunks
        wanted = perm_ref[:, columns(chunk)]
        source = lax.broadcasted_iota(jnp.int32, (width, width), 0) + block * width
        onehot[chunk, columns(block), :] = jnp.where(source == wanted, 1.0, 0.0).astype(bf16)
        return carry

    lax.fori_loop(0, chunks * chunks, fill_onehot, 0)
    fetch_measured.wait()

    def clear(chunk, carry):
        hand_on(SWITCH, chunk, jnp.zeros((full, width_b), f32))
        return carry

    lax.fori_loop(0, chunks_b, clear, 0)

    def arrive(level, chunk):
        remote(level, chunk).wait_recv()
        return product(1 + level, stage(level)[1][chunk])

    def when_in_range(chunk, body, chunks=chunks):
        pl.when(jnp.logical_and(chunk >= 0, chunk < chunks))(lambda: body(chunk))

    def level_0(chunk):
        hand_on(1, chunk, arrive(0, chunk))
        remote(1, chunk).start()

    def level_1(chunk):
        hand_on(2, chunk, arrive(1, chunk))

    def level_2(chunk):
        hand_on(3, chunk, arrive(2, chunk))
        remote(3, chunk).start()

    def take(chunk):
        coeffs = arrive(3, chunk)
        high = coeffs.astype(bf16)
        parts[:full] = high
        parts[full:] = (coeffs - high.astype(f32)).astype(bf16)

    def place(chunk, target):
        both = jnp.dot(parts[...], onehot[target, columns(chunk), :], preferred_element_type=f32)
        both = both[:full] + both[full:]
        for piece in range(pieces):
            which = target * pieces + piece
            block = both[:, piece * width_b : (piece + 1) * width_b]
            far_out[0, which] += block[:half]
            far_held[0, which, :half] += block[half:]

    def place_from(chunk, first):
        def one(target, carry):
            place(chunk, target)
            return carry

        lax.fori_loop(first, chunks, one, 0, unroll=UNROLL)

    def level_3(chunk):
        take(chunk)
        place_from(chunk, 0)

    def last_level_3():
        take(chunks - 1)
        for target in range(FIRST):
            place(chunks - 1, target)
            for piece in range(pieces):
                remote(SWITCH, target * pieces + piece).start()
        place_from(chunks - 1, FIRST)

    def switch(chunk):
        pl.when(chunk >= FIRST * pieces)(lambda: remote(SWITCH, chunk).start())

    def middle(level, chunk):
        hand_on(level + 1, chunk, arrive(level, chunk))
        remote(level + 1, chunk).start()

    def level_7(chunk):
        coeffs = arrive(7, chunk)
        real, imag = coeffs[:half], coeffs[half:]
        scale = measured[:, columns(chunk, width_b)] * lax.rsqrt(jnp.maximum(real * real + imag * imag, 0.25))
        image[chunk, 0] = real * scale
        image[chunk, 1] = imag * scale
        put_image(chunk).start()

    first_core = grp % 2 == 0

    def send(level, chunk):
        remote(level, chunk).start()

    def near(step, carry):
        when_in_range(step, level_0)
        pl.when(step + EARLY < chunks)(lambda: send(0, step + EARLY))
        when_in_range(step - 1, level_1)
        return carry

    def along(step, carry):
        when_in_range(step, level_2)

        @pl.when(jnp.logical_and(first_core, step == chunks - SPARE))
        def _():
            pl.semaphore_signal(turn_sem, inc=1, device_id=partner(1), device_id_type=MESH)

        when_in_range(step - LAG_3, level_3, chunks - 1)
        return carry

    @pl.when(first_core)
    def _():
        def both(step, carry):
            near(step, carry)
            when_in_range(step - 1, functools.partial(send, 2))
            return along(step - LAG_2, carry)

        lax.fori_loop(0, chunks - 1 + LAG_2 + LAG_3, both, 0)

    @pl.when(jnp.logical_not(first_core))
    def _():
        def open_turn():
            for chunk in range(AHEAD):
                send(2, chunk)

        lax.fori_loop(0, chunks + 1, near, 0)
        if BEFORE:
            open_turn()
        pl.semaphore_wait(turn_sem, 1)
        if not BEFORE:
            open_turn()

        def rest(step, carry):
            along(step, carry)
            pl.when(step + AHEAD < chunks)(lambda: send(2, step + AHEAD))
            return carry

        lax.fori_loop(0, chunks - 1 + LAG_3, rest, 0)

    last_level_3()

    def leave(levels, chunk):
        for level in levels:
            remote(level, chunk).wait_send()

    lags = (0, LAG_4, LAG_4 + LAG_5, LAG_4 + LAG_5 + LAG_6, LAG_4 + LAG_5 + LAG_6 + LAG_7)

    def across(step, carry):
        when_in_range(step, switch, chunks_b)
        when_in_range(step - lags[1], functools.partial(middle, 4), chunks_b)
        when_in_range(step - lags[2], functools.partial(middle, 5), chunks_b)
        when_in_range(step - lags[3], functools.partial(middle, 6), chunks_b)
        when_in_range(step - lags[4], level_7, chunks_b)
        when_in_range(step, functools.partial(leave, range(SWITCH)))
        when_in_range(step - lags[4], functools.partial(leave, range(SWITCH, LEVELS)), chunks_b)
        return carry

    lax.fori_loop(0, chunks_b + lags[4], across, 0)

    def finish(chunk, carry):
        put_image(chunk).wait()
        return carry

    lax.fori_loop(0, chunks_b, finish, 0)


def pass_on(source, target, buffer, in_sem, out_sem):
    parts, _, rows, _ = buffer.shape
    for part in range(parts):
        where = pl.ds(part * rows, rows)
        pltpu.make_async_copy(source.at[0, :, where], buffer.at[part], in_sem.at[part]).start()
    for part in range(parts):
        where = pl.ds(part * rows, rows)
        pltpu.make_async_copy(source.at[0, :, where], buffer.at[part], in_sem.at[part]).wait()
        pltpu.make_async_copy(buffer.at[part], target.at[0, :, where], out_sem.at[part]).start()
    for part in range(parts):
        where = pl.ds(part * rows, rows)
        pltpu.make_async_copy(buffer.at[part], target.at[0, :, where], out_sem.at[part]).wait()


def solution(mesh):
    dev_bits = mesh.shape["dev"].bit_length() - 1

    def per_device(wavefield, measured, leaf_map, factors, closing, box_perm, factor_order):
        _, _, half, boxes = wavefield.shape
        width, width_b = min(WIDTH, boxes), min(WIDTH_B, boxes)
        chunks, chunks_b = boxes // width, boxes // width_b
        full = 2 * half
        f32, bf16 = jnp.float32, jnp.bfloat16
        in_hbm = pl.BlockSpec(memory_space=pltpu.HBM)
        in_vmem = pl.BlockSpec(memory_space=pltpu.VMEM)
        image = pl.pallas_call(
            functools.partial(kernel, dev_bits),
            out_shape=jax.ShapeDtypeStruct(wavefield.shape, f32),
            in_specs=[
                pl.BlockSpec(memory_space=pltpu.SMEM),
                in_vmem,
            ]
            + [in_hbm] * 5,
            out_specs=in_hbm,
            scratch_shapes=[
                pltpu.VMEM((2, half, boxes), f32),
                pltpu.VMEM((half, boxes), f32),
                pltpu.VMEM((2, half, half), f32),
                pltpu.VMEM((LEVELS, 2, half, half), f32),
                pltpu.VMEM((2, half, half), f32),
                pltpu.VMEM((LEVELS + 1, 2 * full, full), bf16),
                pltpu.VMEM((chunks, boxes, width), bf16),
                pltpu.VMEM((SWITCH, chunks, half, width), f32),
                pltpu.VMEM((SWITCH, chunks, full, width), f32),
                pltpu.VMEM((LEVELS - SWITCH, chunks_b, half, width_b), f32),
                pltpu.VMEM((LEVELS - SWITCH, chunks_b, full, width_b), f32),
                pltpu.VMEM((2 * full, width), bf16),
                pltpu.VMEM((chunks_b, 2, half, width_b), f32),
                pltpu.SemaphoreType.DMA((4,)),
                pltpu.SemaphoreType.DMA((chunks,)),
                pltpu.SemaphoreType.DMA((SWITCH, chunks)),
                pltpu.SemaphoreType.DMA((SWITCH, chunks)),
                pltpu.SemaphoreType.DMA((LEVELS - SWITCH, chunks_b)),
                pltpu.SemaphoreType.DMA((LEVELS - SWITCH, chunks_b)),
                pltpu.SemaphoreType.DMA((chunks_b,)),
                pltpu.SemaphoreType.REGULAR,
            ],
            compiler_params=pltpu.CompilerParams(
                collective_id=0, has_side_effects=True, vmem_limit_bytes=VMEM_BYTES
            ),
        )(factor_order, box_perm, wavefield, measured, leaf_map, factors, closing)
        return pl.pallas_call(
            pass_on,
            out_shape=jax.ShapeDtypeStruct(wavefield.shape, f32),
            in_specs=[in_hbm],
            out_specs=in_hbm,
            scratch_shapes=[
                pltpu.VMEM((half // ROWS, 2, ROWS, boxes), f32),
                pltpu.SemaphoreType.DMA((half // ROWS,)),
                pltpu.SemaphoreType.DMA((half // ROWS,)),
            ],
            compiler_params=pltpu.CompilerParams(vmem_limit_bytes=VMEM_BYTES),
        )(image)

    return jax.shard_map(
        per_device,
        mesh=mesh,
        in_specs=(
            P(("grp", "dev"), None, None, None),
            P(("grp", "dev"), None, None),
            P(("grp", "dev"), None, None, None),
            P(None, ("grp", "dev"), None, None, None),
            P(("grp", "dev"), None, None, None),
            P(("grp", "dev"), None),
            P(),
        ),
        out_specs=P(("grp", "dev"), None, None, None),
        check_vma=False,
    )
```

```python
import functools

import jax
import jax.numpy as jnp
from jax import lax
from jax.experimental import pallas as pl
from jax.experimental.pallas import tpu as pltpu
from jax.sharding import PartitionSpec as P

MESH = pl.DeviceIdType.MESH
LEVELS = 8
VMEM_BYTES = 67043328
SWITCH = LEVELS // 2
WIDTH = 256
WIDTH_B = 128
EARLY = 5
AHEAD = 3
SPARE = 1
BEFORE = 0
LAG_2 = 3
LAG_3 = 3
ROWS = 16
FIRST = 2
UNROLL = 2
LAG_4 = 2
LAG_5 = 3
LAG_6 = 3
LAG_7 = 3


def kernel(
    dev_bits, order_ref, perm_ref, field_hbm, measured_hbm, leaf_hbm, factors_hbm, closing_hbm, image_hbm,
    field, measured, leaf, factors, closing, weights, onehot, near_out, near_held, far_out, far_held, parts, image,
    in_sem, chunk_sem, near_send, near_recv, far_send, far_recv, out_sem, turn_sem,
):
    chunks, half, width = near_out.shape[1:]
    chunks_b, _, width_b = far_out.shape[1:]
    pieces = width // width_b
    slots = half // 2
    full = 2 * half
    f32, bf16 = jnp.float32, jnp.bfloat16
    grp, dev = lax.axis_index("grp"), lax.axis_index("dev")

    def bit_of(level):
        if level < 2:
            return (grp // (2 >> level)) % 2
        return (dev // (1 << (level - 2) % dev_bits)) % 2

    bits = [bit_of(level) for level in range(LEVELS)]

    def partner(level):
        turn = 1 - 2 * bits[level]
        if level < 2:
            return (grp + turn * (2 >> level), dev)
        return (grp, dev + turn * (1 << (level - 2) % dev_bits))

    def columns(chunk, width=width):
        return pl.ds(pl.multiple_of(chunk * width, width), width)

    def stage(level):
        if level < SWITCH:
            return near_out.at[level], near_held.at[level], near_send.at[level], near_recv.at[level]
        level -= SWITCH
        return far_out.at[level], far_held.at[level], far_send.at[level], far_recv.at[level]

    def remote(level, chunk):
        outgoing, held, send_sem, recv_sem = stage(level)
        return pltpu.make_async_remote_copy(
            src_ref=outgoing.at[chunk],
            dst_ref=held.at[chunk, pl.ds(half, half)],
            send_sem=send_sem.at[chunk],
            recv_sem=recv_sem.at[chunk],
            device_id=partner(level),
            device_id_type=MESH,
        )

    def fetch_field(chunk):
        return pltpu.make_async_copy(
            field_hbm.at[0, :, :, columns(chunk)], field.at[:, :, columns(chunk)], chunk_sem.at[chunk]
        )

    def put_image(chunk):
        return pltpu.make_async_copy(
            image.at[chunk], image_hbm.at[0, :, :, columns(chunk, width_b)], out_sem.at[chunk]
        )

    barrier = pltpu.get_barrier_semaphore()
    for level in range(LEVELS):
        pl.semaphore_signal(barrier, inc=1, device_id=partner(level), device_id_type=MESH)

    fetch_leaf = pltpu.make_async_copy(leaf_hbm.at[0], leaf, in_sem.at[0])
    fetch_leaf.start()
    for chunk in range(chunks):
        fetch_field(chunk).start()
    fetch_factors = pltpu.make_async_copy(factors_hbm.at[:, 0], factors, in_sem.at[1])
    fetch_factors.start()
    fetch_closing = pltpu.make_async_copy(closing_hbm.at[0], closing, in_sem.at[2])
    fetch_closing.start()
    fetch_measured = pltpu.make_async_copy(measured_hbm.at[0], measured, in_sem.at[3])
    fetch_measured.start()

    def store_weights(which, row, left, right):
        rows = left.shape[0]
        for side, block in ((0, left), (half, right)):
            high = block.astype(bf16)
            low = (block - high.astype(f32)).astype(bf16)
            weights[which, row : row + rows, side : side + half] = high
            weights[which, full + row : full + row + rows, side : side + half] = low

    def prepare(which, load, in_bit, out_bit):
        if out_bit is None:
            blocks = [(0, half, 0, half)]
        else:
            blocks = [
                (0, slots, (1 - out_bit) * slots, slots),
                (half, half + slots, out_bit * slots, slots),
            ]
        for real_row, imag_row, start, rows in blocks:
            if not isinstance(start, int):
                start = pl.multiple_of(start, slots)
            real = load(0, pl.ds(start, rows))
            imag = load(1, pl.ds(start, rows))
            if in_bit is None:
                store_weights(which, real_row, real, -imag)
                store_weights(which, imag_row, imag, real)
            else:
                first = lax.broadcasted_iota(jnp.int32, real.shape, 1) < slots
                real_over, imag_over = pltpu.roll(real, slots, 1), pltpu.roll(imag, slots, 1)
                own_first = in_bit == 0
                real, real_over = jnp.where(own_first, real, real_over), jnp.where(own_first, real_over, real)
                imag, imag_over = jnp.where(own_first, imag, imag_over), jnp.where(own_first, imag_over, imag)
                store_weights(
                    which, real_row, jnp.where(first, real, -imag_over), jnp.where(first, real_over, -imag)
                )
                store_weights(
                    which, imag_row, jnp.where(first, imag, real_over), jnp.where(first, imag_over, real)
                )

    def product(which, vectors):
        high = vectors.astype(bf16)
        low = (vectors - high.astype(f32)).astype(bf16)
        count = vectors.shape[1]
        if count <= 128:
            all_four = jnp.dot(weights[which], jnp.concatenate([high, low], axis=1), preferred_element_type=f32)
            return all_four[:full, :count] + (all_four[full:, :count] + all_four[:full, count:])
        both = jnp.dot(weights[which], high, preferred_element_type=f32)
        rest = jnp.dot(weights[which, :full], low, preferred_element_type=f32)
        return both[:full] + (both[full:] + rest)

    def hand_on(level, chunk, coeffs):
        outgoing, held, _, _ = stage(level)
        outgoing[chunk] = coeffs[:half]
        held[chunk, :half] = coeffs[half:]

    fetch_leaf.wait()
    prepare(0, lambda part, rows: leaf[part, rows, :], None, bits[0])
    pl.semaphore_wait(barrier, LEVELS)

    def open_chunk(chunk, carry):
        fetch_field(chunk).wait()
        vectors = field[:, :, columns(chunk)].reshape(full, width)
        hand_on(0, chunk, product(0, vectors))
        pl.when(chunk < EARLY)(lambda: remote(0, chunk).start())
        return carry

    lax.fori_loop(0, chunks, open_chunk, 0)

    fetch_factors.wait()
    fetch_closing.wait()
    for level in range(LEVELS):
        pick = order_ref[level]
        prepare(
            1 + level,
            lambda part, rows, pick=pick: factors[pick, part, rows, :],
            bits[level],
            bits[level + 1] if level + 1 < LEVELS else None,
        )
    prepare(0, lambda part, rows: closing[part, rows, :], None, None)
    last = weights[LEVELS, :full].astype(f32) + weights[LEVELS, full:].astype(f32)
    last = product(0, last)
    high = last.astype(bf16)
    weights[LEVELS, :full] = high
    weights[LEVELS, full:] = (last - high.astype(f32)).astype(bf16)

    def fill_onehot(step, carry):
        chunk, block = step // chunks, step % chunks
        wanted = perm_ref[:, columns(chunk)]
        source = lax.broadcasted_iota(jnp.int32, (width, width), 0) + block * width
        onehot[chunk, columns(block), :] = jnp.where(source == wanted, 1.0, 0.0).astype(bf16)
        return carry

    lax.fori_loop(0, chunks * chunks, fill_onehot, 0)
    fetch_measured.wait()

    def clear(chunk, carry):
        hand_on(SWITCH, chunk, jnp.zeros((full, width_b), f32))
        return carry

    lax.fori_loop(0, chunks_b, clear, 0)

    def arrive(level, chunk):
        remote(level, chunk).wait_recv()
        return product(1 + level, stage(level)[1][chunk])

    def when_in_range(chunk, body, chunks=chunks):
        pl.when(jnp.logical_and(chunk >= 0, chunk < chunks))(lambda: body(chunk))

    def level_0(chunk):
        hand_on(1, chunk, arrive(0, chunk))
        remote(1, chunk).start()

    def level_1(chunk):
        hand_on(2, chunk, arrive(1, chunk))

    def level_2(chunk):
        hand_on(3, chunk, arrive(2, chunk))
        remote(3, chunk).start()

    def take(chunk):
        coeffs = arrive(3, chunk)
        high = coeffs.astype(bf16)
        parts[:full] = high
        parts[full:] = (coeffs - high.astype(f32)).astype(bf16)

    def place(chunk, target):
        both = jnp.dot(parts[...], onehot[target, columns(chunk), :], preferred_element_type=f32)
        both = both[:full] + both[full:]
        for piece in range(pieces):
            which = target * pieces + piece
            block = both[:, piece * width_b : (piece + 1) * width_b]
            far_out[0, which] += block[:half]
            far_held[0, which, :half] += block[half:]

    def place_from(chunk, first):
        def one(target, carry):
            place(chunk, target)
            return carry

        lax.fori_loop(first, chunks, one, 0, unroll=UNROLL)

    def level_3(chunk):
        take(chunk)
        place_from(chunk, 0)

    def last_level_3():
        take(chunks - 1)
        for target in range(FIRST):
            place(chunks - 1, target)
            for piece in range(pieces):
                remote(SWITCH, target * pieces + piece).start()
        place_from(chunks - 1, FIRST)

    def switch(chunk):
        pl.when(chunk >= FIRST * pieces)(lambda: remote(SWITCH, chunk).start())

    def middle(level, chunk):
        hand_on(level + 1, chunk, arrive(level, chunk))
        remote(level + 1, chunk).start()

    def level_7(chunk):
        coeffs = arrive(7, chunk)
        real, imag = coeffs[:half], coeffs[half:]
        scale = measured[:, columns(chunk, width_b)] * lax.rsqrt(jnp.maximum(real * real + imag * imag, 0.25))
        image[chunk, 0] = real * scale
        image[chunk, 1] = imag * scale
        put_image(chunk).start()

    first_core = grp % 2 == 0

    def send(level, chunk):
        remote(level, chunk).start()

    def near(step, carry):
        when_in_range(step, level_0)
        pl.when(step + EARLY < chunks)(lambda: send(0, step + EARLY))
        when_in_range(step - 1, level_1)
        return carry

    def along(step, carry):
        when_in_range(step, level_2)

        @pl.when(jnp.logical_and(first_core, step == chunks - SPARE))
        def _():
            pl.semaphore_signal(turn_sem, inc=1, device_id=partner(1), device_id_type=MESH)

        when_in_range(step - LAG_3, level_3, chunks - 1)
        return carry

    @pl.when(first_core)
    def _():
        def both(step, carry):
            near(step, carry)
            when_in_range(step - 1, functools.partial(send, 2))
            return along(step - LAG_2, carry)

        lax.fori_loop(0, chunks - 1 + LAG_2 + LAG_3, both, 0)

    @pl.when(jnp.logical_not(first_core))
    def _():
        def open_turn():
            for chunk in range(AHEAD):
                send(2, chunk)

        lax.fori_loop(0, chunks + 1, near, 0)
        if BEFORE:
            open_turn()
        pl.semaphore_wait(turn_sem, 1)
        if not BEFORE:
            open_turn()

        def rest(step, carry):
            along(step, carry)
            pl.when(step + AHEAD < chunks)(lambda: send(2, step + AHEAD))
            return carry

        lax.fori_loop(0, chunks - 1 + LAG_3, rest, 0)

    last_level_3()

    def leave(levels, chunk):
        for level in levels:
            remote(level, chunk).wait_send()

    lags = (0, LAG_4, LAG_4 + LAG_5, LAG_4 + LAG_5 + LAG_6, LAG_4 + LAG_5 + LAG_6 + LAG_7)

    def across(step, carry):
        when_in_range(step, switch, chunks_b)
        when_in_range(step - lags[1], functools.partial(middle, 4), chunks_b)
        when_in_range(step - lags[2], functools.partial(middle, 5), chunks_b)
        when_in_range(step - lags[3], functools.partial(middle, 6), chunks_b)
        when_in_range(step - lags[4], level_7, chunks_b)
        when_in_range(step, functools.partial(leave, range(SWITCH)))
        when_in_range(step - lags[4], functools.partial(leave, range(SWITCH, LEVELS)), chunks_b)
        return carry

    lax.fori_loop(0, chunks_b + lags[4], across, 0)

    def finish(chunk, carry):
        put_image(chunk).wait()
        return carry

    lax.fori_loop(0, chunks_b, finish, 0)


def pass_on(source, target, buffer, in_sem, out_sem):
    parts, _, rows, _ = buffer.shape
    for part in range(parts):
        where = pl.ds(part * rows, rows)
        pltpu.make_async_copy(source.at[0, :, where], buffer.at[part], in_sem.at[part]).start()
    for part in range(parts):
        where = pl.ds(part * rows, rows)
        pltpu.make_async_copy(source.at[0, :, where], buffer.at[part], in_sem.at[part]).wait()
        pltpu.make_async_copy(buffer.at[part], target.at[0, :, where], out_sem.at[part]).start()
    for part in range(parts):
        where = pl.ds(part * rows, rows)
        pltpu.make_async_copy(buffer.at[part], target.at[0, :, where], out_sem.at[part]).wait()


def solution(mesh):
    dev_bits = mesh.shape["dev"].bit_length() - 1

    def per_device(wavefield, measured, leaf_map, factors, closing, box_perm, factor_order):
        _, _, half, boxes = wavefield.shape
        width, width_b = min(WIDTH, boxes), min(WIDTH_B, boxes)
        chunks, chunks_b = boxes // width, boxes // width_b
        full = 2 * half
        f32, bf16 = jnp.float32, jnp.bfloat16
        in_hbm = pl.BlockSpec(memory_space=pltpu.HBM)
        in_vmem = pl.BlockSpec(memory_space=pltpu.VMEM)
        image = pl.pallas_call(
            functools.partial(kernel, dev_bits),
            out_shape=jax.ShapeDtypeStruct(wavefield.shape, f32),
            in_specs=[
                pl.BlockSpec(memory_space=pltpu.SMEM),
                in_vmem,
            ]
            + [in_hbm] * 5,
            out_specs=in_hbm,
            scratch_shapes=[
                pltpu.VMEM((2, half, boxes), f32),
                pltpu.VMEM((half, boxes), f32),
                pltpu.VMEM((2, half, half), f32),
                pltpu.VMEM((LEVELS, 2, half, half), f32),
                pltpu.VMEM((2, half, half), f32),
                pltpu.VMEM((LEVELS + 1, 2 * full, full), bf16),
                pltpu.VMEM((chunks, boxes, width), bf16),
                pltpu.VMEM((SWITCH, chunks, half, width), f32),
                pltpu.VMEM((SWITCH, chunks, full, width), f32),
                pltpu.VMEM((LEVELS - SWITCH, chunks_b, half, width_b), f32),
                pltpu.VMEM((LEVELS - SWITCH, chunks_b, full, width_b), f32),
                pltpu.VMEM((2 * full, width), bf16),
                pltpu.VMEM((chunks_b, 2, half, width_b), f32),
                pltpu.SemaphoreType.DMA((4,)),
                pltpu.SemaphoreType.DMA((chunks,)),
                pltpu.SemaphoreType.DMA((SWITCH, chunks)),
                pltpu.SemaphoreType.DMA((SWITCH, chunks)),
                pltpu.SemaphoreType.DMA((LEVELS - SWITCH, chunks_b)),
                pltpu.SemaphoreType.DMA((LEVELS - SWITCH, chunks_b)),
                pltpu.SemaphoreType.DMA((chunks_b,)),
                pltpu.SemaphoreType.REGULAR,
            ],
            compiler_params=pltpu.CompilerParams(
                collective_id=0, has_side_effects=True, vmem_limit_bytes=VMEM_BYTES
            ),
        )(factor_order, box_perm, wavefield, measured, leaf_map, factors, closing)
        return pl.pallas_call(
            pass_on,
            out_shape=jax.ShapeDtypeStruct(wavefield.shape, f32),
            in_specs=[in_hbm],
            out_specs=in_hbm,
            scratch_shapes=[
                pltpu.VMEM((half // ROWS, 2, ROWS, boxes), f32),
                pltpu.SemaphoreType.DMA((half // ROWS,)),
                pltpu.SemaphoreType.DMA((half // ROWS,)),
            ],
            compiler_params=pltpu.CompilerParams(vmem_limit_bytes=VMEM_BYTES),
        )(image)

    return jax.shard_map(
        per_device,
        mesh=mesh,
        in_specs=(
            P(("grp", "dev"), None, None, None),
            P(("grp", "dev"), None, None),
            P(("grp", "dev"), None, None, None),
            P(None, ("grp", "dev"), None, None, None),
            P(("grp", "dev"), None, None, None),
            P(("grp", "dev"), None),
            P(),
        ),
        out_specs=P(("grp", "dev"), None, None, None),
        check_vma=False,
    )
```
